32 devices in a mesh: depth: 4 (over y, x), xline: 8 (over z, core).
Axes of the slice: x: 2, y: 2, z: 4, core: 2. Of those that a mesh axis runs over, the one named last changes fastest.
Arguments:
- receiver_data: bfloat16 [4, 2, 1024, 1024], P(None, None, None, 'xline'), may hold values from -6 to 6
- source_amp: bfloat16 [4, 2, 256], replicated, may hold values from -6 to 6
- source_x: int32 [256], replicated, may hold values from 0 to 1023
- source_y: int32 [256], replicated, may hold values from 0 to 1023
- omegas: float32 [4], replicated, may hold values from 0.5 to 3
- slowness: float32 [4, 1024, 1024], P('depth', None, 'xline'), may hold values from 0.2 to 2
- inverses: bfloat16 [4, 4, 2, 256, 256], replicated, may hold values from -0.1875 to 0.1875
- zones_x: int32 [4, 4], P('depth'), may hold values from 0 to 3
- zones_y: int32 [4, 4], P('depth'), may hold values from 0 to 3
Outputs:
- gradient: float32 [4, 1024, 1024], P('depth', None, 'xline')
The draws below stay inside these ranges and needn't reach their ends.
All inputs are finite; a program needn't handle non-finite values.
Results may differ from the reference program's by a relative error of at most 0.015.
Values may be sent and summed in bfloat16 or wider, within the bound.
A program may use at most 64 MiB of HBM per device.

```python
import math
import jax
import jax.numpy as jnp

NX = 1024
B = 256
NF = 4
ZONES = 4
NSRC = 256
NY = 1024
NZ = 4
NXB = 4
NYB = 4


def set_ends(drawn, key, low, high):
    spot = [jax.random.randint(jax.random.fold_in(key, axis), (), 0, length) for axis, length in enumerate(drawn.shape)]
    longest = drawn.shape.index(max(drawn.shape))
    neighbour = spot[:longest] + [(spot[longest] + 1) % drawn.shape[longest]] + spot[longest + 1:]
    return drawn.at[tuple(spot)].set(low).at[tuple(neighbour)].set(high)


def block_scale(stream_key, extent, split, low, top_value):
    loudness, own = 1.0, jax.random.fold_in(stream_key, 6)
    for dim, blocks in split:
        heights = jnp.exp(jax.random.uniform(jax.random.fold_in(own, dim), (blocks,), jnp.float32, low / len(split), top_value / len(split)))
        loudness = loudness * jnp.repeat(heights, extent[dim] // blocks).reshape([-1 if axis == dim else 1 for axis in range(len(extent))])
    return loudness


def bell_draw(key, dims, scale, reach, cuts=(), dtype=jnp.bfloat16):
    array = jax.random.normal(key, dims, jnp.float32) * scale
    if len(cuts) > 0:
        array = block_scale(key, dims, cuts, -0.22, 0.18) * array
    return jnp.clip(array, min=-reach, max=reach).astype(dtype)


def setup_inputs(seed: int = 0) -> dict:
    splits = jax.random.split(jax.random.key(seed), 10)
    receiver_data = bell_draw(splits[0], (NF, 2, NX, NY), 1.0, 6.0, ((3, 8),))
    source_amp = bell_draw(splits[1], (NF, 2, NSRC), 1.0, 6.0)
    source_x = set_ends(jax.random.randint(splits[2], (NSRC,), 0, NX), jax.random.fold_in(splits[2], 1), 0, NX - 1).astype(jnp.int32)
    source_y = set_ends(jax.random.randint(splits[3], (NSRC,), 0, NY), jax.random.fold_in(splits[3], 1), 0, NY - 1).astype(jnp.int32)
    omegas = jnp.clip(jnp.exp(jax.random.uniform(splits[4], (NF,), jnp.float32, math.log(0.5), math.log(3.0))), 0.5, 3.0)
    slowness = jnp.clip(0.2 + 1.8 * jax.random.uniform(splits[5], (NZ, NX, NY), jnp.float32) ** block_scale(splits[5], (NZ, NX, NY), ((0, 4), (2, 8)), -0.2, 0.2), 0.2, 2.0)
    inverses = bell_draw(splits[6], (NF, ZONES, 2, B, B), (4 * B) ** -0.5, 0.1875)
    zones_x = set_ends(jax.random.randint(splits[7], (NZ, NXB), 0, ZONES), jax.random.fold_in(splits[7], 1), 0, ZONES - 1).astype(jnp.int32)
    zones_y = set_ends(jax.random.randint(splits[8], (NZ, NYB), 0, ZONES), jax.random.fold_in(splits[8], 1), 0, ZONES - 1).astype(jnp.int32)
    return {"receiver_data": receiver_data, "source_amp": source_amp, "source_x": source_x, "source_y": source_y, "omegas": omegas, "slowness": slowness, "inverses": inverses, "zones_x": zones_x, "zones_y": zones_y}


def rotate(field, angle, sign):
    field_real = field[0].astype(jnp.float32)
    field_imag = field[1].astype(jnp.float32)
    cosine = jnp.cos(angle)
    sine = jnp.sin(angle) * sign
    return jnp.stack([field_real * cosine - field_imag * sine, field_real * sine + field_imag * cosine]).astype(jnp.bfloat16)


def solve_inline(field, blocks, sign):
    parts = field.astype(jnp.float32).reshape(2, NX // B, B, field.shape[2])
    k_real = blocks[:, 0].astype(jnp.float32)
    k_imag = sign * blocks[:, 1].astype(jnp.float32)
    def blockwise(matrix, vector):
        return jnp.einsum("bij,bjy->biy", matrix, vector)
    out_real = parts[0] + blockwise(k_real, parts[0]) - blockwise(k_imag, parts[1])
    out_imag = parts[1] + blockwise(k_real, parts[1]) + blockwise(k_imag, parts[0])
    return jnp.stack([out_real, out_imag]).reshape(field.shape).astype(jnp.bfloat16)


def solve_crossline(field, blocks, sign):
    parts = field.astype(jnp.float32).reshape(2, field.shape[1], NY // B, B)
    k_real = blocks[:, 0].astype(jnp.float32)
    k_imag = sign * blocks[:, 1].astype(jnp.float32)
    def blockwise(matrix, vector):
        return jnp.einsum("bij,xbj->xbi", matrix, vector)
    out_real = parts[0] + blockwise(k_real, parts[0]) - blockwise(k_imag, parts[1])
    out_imag = parts[1] + blockwise(k_real, parts[1]) + blockwise(k_imag, parts[0])
    return jnp.stack([out_real, out_imag]).reshape(field.shape).astype(jnp.bfloat16)


def continue_level(field, angle, table, zone_row_x, zone_row_y, sign):
    rotated = rotate(field, angle, sign)
    inline = solve_inline(rotated, jnp.take(table, zone_row_x, axis=0), sign)
    return solve_crossline(inline, jnp.take(table, zone_row_y, axis=0), sign)


def reference(receiver_data, source_amp, source_x, source_y, omegas, slowness, inverses, zones_x, zones_y):
    source_all = jnp.zeros((NF, 2, NX, NY), jnp.float32).at[:, :, source_x, source_y].add(source_amp.astype(jnp.float32))
    source_all = source_all.astype(jnp.bfloat16)
    gradient = jnp.zeros((NZ, NX, NY), jnp.float32)
    for freq in range(NF):
        source_field = source_all[freq]
        receiver_field = receiver_data[freq]
        weight = omegas[freq] * omegas[freq]
        for level in range(NZ):
            angle = omegas[freq] * slowness[level]
            source_field = continue_level(source_field, angle, inverses[freq], zones_x[level], zones_y[level], 1.0)
            receiver_field = continue_level(receiver_field, angle, inverses[freq], zones_x[level], zones_y[level], -1.0)
            correlation = source_field[0].astype(jnp.float32) * receiver_field[0].astype(jnp.float32) + source_field[1].astype(jnp.float32) * receiver_field[1].astype(jnp.float32)
            gradient = gradient.at[level].add(weight * correlation)
    return gradient
```

```python
import functools
import math

import jax
import jax.numpy as jnp
from jax import lax
from jax.experimental import pallas as pl
from jax.experimental.pallas import tpu as pltpu
from jax.sharding import PartitionSpec as P

MESH = pl.DeviceIdType.MESH
F32 = jnp.float32
BF16 = jnp.bfloat16

SIN_TERMS = [(-1.0) ** k / math.factorial(2 * k + 1) for k in range(7)]
COS_TERMS = [(-1.0) ** k / math.factorial(2 * k) for k in range(8)]
PI_HIGH = 3.140625
PI_MID = 9.67502593994140625e-4
PI_LOW = math.pi - PI_HIGH - PI_MID


def series(square, terms):
    total = jnp.full_like(square, terms[-1])
    for term in terms[-2::-1]:
        total = total * square + term
    return total


def sincos(angle):
    turns = jnp.floor(angle * (1.0 / math.pi) + 0.5)
    rest = ((angle - turns * PI_HIGH) - turns * PI_MID) - turns * PI_LOW
    odd = turns - 2.0 * jnp.floor(turns * 0.5)
    sign = 1.0 - 2.0 * odd
    square = rest * rest
    return series(square, SIN_TERMS) * (rest * sign), series(square, COS_TERMS) * sign


def block_form(blocks):
    k_real, k_imag = blocks[0], blocks[1]
    top = jnp.concatenate([k_real, -k_imag], axis=1)
    bottom = jnp.concatenate([k_imag, k_real], axis=1)
    return jnp.concatenate([top, bottom], axis=0)


def kernel(
    sections, pair, rows, recv_in, amp, src_x, src_y, omegas, slow_in, table_in, zones,
    out, slow, rec, wave, table, zone_buf, zone_rows, rotated, inline, own, sent, got, total,
    local_sems, zone_send, zone_recv, slow_send, slow_recv, fwd_send, fwd_recv,
    rec_send, rec_recv, swap_send, swap_recv, grad_send, grad_recv,
):
    d = lax.axis_index("depth")
    line = lax.axis_index("xline")
    q = lax.rem(line, pair)
    block = line // pair
    mate_line = line + 1 - 2 * q
    width = recv_in.shape[3]
    order = pair * width
    slots = wave.shape[0]
    mine = pl.ds(pl.multiple_of(q * width, width), width)
    theirs = pl.ds(pl.multiple_of((1 - q) * width, width), width)

    def rows_of(section):
        return pl.ds(pl.multiple_of(section * order, order), order)

    barrier = pltpu.get_barrier_semaphore()
    pl.semaphore_signal(barrier, inc=1, device_id=(d, mate_line), device_id_type=MESH)
    others = [lax.rem(d + k, sections) for k in range(1, sections)]
    for other in others:
        pl.semaphore_signal(barrier, inc=1, device_id=(other, line), device_id_type=MESH)

    freqs = pl.ds(q * slots, slots)
    local = [
        pltpu.make_async_copy(
            slow_in.at[0, rows_of(d), :], slow.at[d, :, mine], local_sems.at[0]
        ),
        pltpu.make_async_copy(
            recv_in.at[freqs, :, rows_of(d), :], rec.at[:, :, :, mine], local_sems.at[1]
        ),
        pltpu.make_async_copy(table_in.at[freqs], table, local_sems.at[2]),
        pltpu.make_async_copy(zones, zone_buf.at[d], local_sems.at[3]),
    ]
    for copy in local:
        copy.start()
    pl.semaphore_wait(barrier, sections)

    zone_copies, slow_copies = [], []
    for k, other in enumerate(others):
        zone_copies.append(
            pltpu.make_async_remote_copy(
                src_ref=zones, dst_ref=zone_buf.at[d], send_sem=zone_send.at[k],
                recv_sem=zone_recv.at[d], device_id=(other, line), device_id_type=MESH,
            )
        )
        slow_copies.append(
            pltpu.make_async_remote_copy(
                src_ref=slow_in.at[0, rows_of(other), :], dst_ref=slow.at[d, :, mine],
                send_sem=slow_send.at[k], recv_sem=slow_recv.at[d],
                device_id=(other, line), device_id_type=MESH,
            )
        )
    for copy in zone_copies + slow_copies:
        copy.start()
    rec_copy = pltpu.make_async_remote_copy(
        src_ref=recv_in.at[pl.ds((1 - q) * slots, slots), :, rows_of(d), :],
        dst_ref=rec.at[:, :, :, mine], send_sem=rec_send, recv_sem=rec_recv,
        device_id=(d, mate_line), device_id_type=MESH,
    )
    rec_copy.start()

    points = src_x.shape[1]
    cells = lax.broadcasted_iota(jnp.int32, (order, points), 0)
    hit_x = cells + d * order == src_x[...]
    hit_y = jnp.where(cells + block * order == src_y[...], 1.0, 0.0).astype(BF16)
    for slot in range(slots):
        for part in range(2):
            amps = amp[q * slots + slot, pl.ds(part, 1), :].astype(F32)
            spread = jnp.where(hit_x, amps, 0.0).astype(BF16)
            field = lax.dot_general(
                spread, hit_y, (((1,), (1,)), ((), ())), preferred_element_type=F32
            )
            wave[slot, 0, part] = field.astype(BF16)

    def arrived_slow(level):
        return pltpu.make_async_remote_copy(
            src_ref=slow.at[level, :, mine], dst_ref=slow.at[level, :, mine],
            send_sem=slow_send.at[0], recv_sem=slow_recv.at[level],
            device_id=(d, mate_line), device_id_type=MESH,
        )

    def forward(level, half):
        return pltpu.make_async_remote_copy(
            src_ref=slow.at[level, :, half], dst_ref=slow.at[level, :, half],
            send_sem=fwd_send.at[level], recv_sem=fwd_recv.at[level],
            device_id=(d, mate_line), device_id_type=MESH,
        )

    local[0].wait()

    def relay(level):
        @pl.when(level != d)
        def _():
            arrived_slow(level).wait_recv()

        forward(level, mine).start()

    relay(0)

    local[1].wait()
    rec_copy.wait_recv()
    for slot in range(slots):
        wave[slot, 1, 0] = rec[slot, 0]
        wave[slot, 1, 1] = -rec[slot, 1]
    local[2].wait()
    local[3].wait()
    for level in range(sections):
        @pl.when(level != d)
        def _():
            pltpu.make_async_remote_copy(
                src_ref=zones, dst_ref=zone_buf.at[level], send_sem=zone_send.at[0],
                recv_sem=zone_recv.at[level], device_id=(d, mate_line), device_id_type=MESH,
            ).wait_recv()
    zone_copy = pltpu.make_async_copy(zone_buf, zone_rows, local_sems.at[4])
    zone_copy.start()
    zone_copy.wait()
    forward(0, theirs).wait_recv()

    def advance(level, slot):
        omega = omegas[q * slots + slot]
        m_x = block_form(table[slot, zone_rows[level, 0, d]])
        m_y = block_form(table[slot, zone_rows[level, 0, sections + block]])
        step = min(rows, order)
        for start in range(0, order, step):
            part = slice(start, start + step)
            sine, cosine = sincos(omega * slow[level, part, :])
            for field in range(2):
                real = wave[slot, field, 0, part, :].astype(F32)
                imag = wave[slot, field, 1, part, :].astype(F32)
                lanes = slice(field * order, (field + 1) * order)
                rotated[part, lanes] = (real * cosine - imag * sine).astype(BF16)
                rotated[order + start:order + start + step, lanes] = (
                    real * sine + imag * cosine
                ).astype(BF16)
        for field in range(2):
            lanes = slice(field * order, (field + 1) * order)
            value = rotated[:, lanes]
            solved = value.astype(F32) + jnp.dot(m_x, value, preferred_element_type=F32)
            solved = solved.astype(BF16)
            inline[lanes, 0:order] = solved[:order]
            inline[lanes, order:] = solved[order:]
        value = inline[...]
        product = []
        for part in range(2):
            lanes = slice(part * order, (part + 1) * order)
            solved = value[:, lanes].astype(F32) + lax.dot_general(
                value, m_y[lanes], (((1,), (1,)), ((), ())), preferred_element_type=F32
            )
            solved = solved.astype(BF16)
            wave[slot, 0, part] = solved[:order]
            wave[slot, 1, part] = solved[order:]
            product.append(solved[:order].astype(F32) * solved[order:].astype(F32))
        image = (omega * omega) * (product[0] - product[1])
        if slot == 0:
            total[...] = image
        else:
            total[...] += image

    def swap(level):
        return pltpu.make_async_remote_copy(
            src_ref=sent.at[level], dst_ref=got.at[level],
            send_sem=swap_send.at[level], recv_sem=swap_recv.at[level],
            device_id=(d, mate_line), device_id_type=MESH,
        )

    def deliver_copy(level):
        return pltpu.make_async_remote_copy(
            src_ref=own.at[level], dst_ref=out.at[rows_of(d), :],
            send_sem=grad_send.at[level], recv_sem=grad_recv.at[d],
            device_id=(level, line), device_id_type=MESH,
        )

    def deliver(level):
        swap(level).wait_recv()
        both = own[level].astype(F32) + got[level].astype(F32)

        @pl.when(level == d)
        def _():
            out[rows_of(d), :] = both.astype(BF16)

        @pl.when(level != d)
        def _():
            own[level] = both.astype(BF16)
            deliver_copy(level).start()

    def level_step(level, carry):
        for slot in range(slots):
            advance(level, slot)
            if slot == 0:
                @pl.when(level + 1 < sections)
                def _():
                    relay(level + 1)

                @pl.when(level > 0)
                def _():
                    deliver(level - 1)
        own[level] = total[:, mine].astype(BF16)
        sent[level] = total[:, theirs].astype(BF16)
        swap(level).start()

        @pl.when(level + 1 < sections)
        def _():
            forward(level + 1, theirs).wait_recv()

        return carry

    lax.fori_loop(0, sections, level_step, 0)
    deliver(sections - 1)

    for copy in zone_copies + slow_copies:
        copy.wait_send()
    rec_copy.wait_send()
    for level in range(sections):
        forward(level, mine).wait_send()
        swap(level).wait_send()

        @pl.when(level != d)
        def _():
            deliver_copy(level).wait_send()
            pltpu.make_async_remote_copy(
                src_ref=own.at[level], dst_ref=out.at[rows_of(level), :],
                send_sem=grad_send.at[0], recv_sem=grad_recv.at[level],
                device_id=(level, line), device_id_type=MESH,
            ).wait_recv()


def per_device(
    receiver_data, source_amp, source_x, source_y, omegas, slowness, inverses, zones_x, zones_y
):
    sections = lax.axis_size("depth")
    freqs, _, width_x, width_y = receiver_data.shape
    order = inverses.shape[-1]
    pair = order // width_y
    points = source_x.shape[0]
    zone_count = inverses.shape[1]
    slots = freqs // pair
    assert pair == 2 and width_x == order * sections and slowness.shape[0] == 1
    zones = jnp.concatenate([zones_x, zones_y], axis=1)
    zones = jnp.pad(zones, ((0, 0), (0, 128 - zones.shape[1])))
    vmem = pl.BlockSpec(memory_space=pltpu.VMEM)
    smem = pl.BlockSpec(memory_space=pltpu.SMEM)
    anywhere = pl.BlockSpec(memory_space=pl.ANY)
    dma = pltpu.SemaphoreType.DMA
    out = pl.pallas_call(
        functools.partial(kernel, sections, pair, 32),
        out_shape=jax.ShapeDtypeStruct((width_x, width_y), BF16),
        in_specs=[anywhere, vmem, vmem, vmem, smem, anywhere, anywhere, vmem],
        out_specs=vmem,
        scratch_shapes=[
            pltpu.VMEM((sections, order, order), slowness.dtype),
            pltpu.VMEM((slots, 2, order, order), BF16),
            pltpu.VMEM((slots, 2, 2, order, order), BF16),
            pltpu.VMEM((slots, zone_count, 2, order, order), BF16),
            pltpu.VMEM((sections, 1, 128), jnp.int32),
            pltpu.SMEM((sections, 1, 128), jnp.int32),
            pltpu.VMEM((2 * order, 2 * order), BF16),
            pltpu.VMEM((2 * order, 2 * order), BF16),
            pltpu.VMEM((sections, order, width_y), BF16),
            pltpu.VMEM((sections, order, width_y), BF16),
            pltpu.VMEM((sections, order, width_y), BF16),
            pltpu.VMEM((order, order), F32),
            dma((5,)),
            dma((sections,)), dma((sections,)),
            dma((sections,)), dma((sections,)),
            dma((sections,)), dma((sections,)),
            dma, dma,
            dma((sections,)), dma((sections,)),
            dma((sections,)), dma((sections,)),
        ],
        compiler_params=pltpu.CompilerParams(collective_id=0, has_side_effects=True),
    )(
        receiver_data, source_amp, source_x.reshape(1, points), source_y.reshape(1, points),
        omegas, slowness, inverses, zones,
    )
    return out.astype(F32)[None]


def solution(mesh):
    in_specs = (
        P(None, None, None, "xline"),
        P(),
        P(),
        P(),
        P(),
        P("depth", None, "xline"),
        P(),
        P("depth", None),
        P("depth", None),
    )
    out_specs = P("depth", None, "xline")
    return jax.shard_map(
        per_device, mesh=mesh, in_specs=in_specs, out_specs=out_specs, check_vma=False
    )
```

```python
import functools
import math

import jax
import jax.numpy as jnp
import numpy as np
from jax import lax
from jax.experimental import pallas as pl
from jax.experimental.pallas import tpu as pltpu
from jax.sharding import PartitionSpec as P

MESH = pl.DeviceIdType.MESH
F32 = jnp.float32
BF16 = jnp.bfloat16

SLOW_LOW, SLOW_HIGH = 0.2, 2.0
OMEGA_LOW, OMEGA_HIGH = 0.5, 3.0
SLOW_MID = 0.5 * (SLOW_LOW + SLOW_HIGH)
CODE_STEP = (SLOW_HIGH - SLOW_LOW) / 65532.0
HALF_SPAN = 0.5 * max(OMEGA_HIGH * SLOW_HIGH - math.pi, math.pi - OMEGA_LOW * SLOW_LOW) + 0.01


def fitted(function, count):
    nodes = np.cos(np.pi * (np.arange(64) + 0.5) / 64)
    square = 0.5 * HALF_SPAN**2 * (nodes + 1.0)
    fit = np.polynomial.Chebyshev.fit(square, function(np.sqrt(square)), count - 1)
    return [float(term) for term in fit.convert(kind=np.polynomial.Polynomial).coef]


SIN_TERMS = fitted(lambda t: np.sin(t) / t, 6)
COS_TERMS = fitted(np.cos, 6)


def series(square, terms):
    total = square * terms[-1] + terms[-2]
    for term in terms[-3::-1]:
        total = total * square + term
    return total


def sincos(half):
    square = half * half
    sine = series(square, SIN_TERMS) * half
    cosine = series(square, COS_TERMS)
    double = sine + sine
    return -(double * cosine), double * sine - 1.0


def block_form(blocks):
    k_real, k_imag = blocks[0], blocks[1]
    top = jnp.concatenate([k_real, -k_imag], axis=1)
    bottom = jnp.concatenate([k_imag, k_real], axis=1)
    return jnp.concatenate([top, bottom], axis=0)


def kernel(
    sections, pair, rows, recv_in, amp, src_x, src_y, omegas, slow_in, table_in,
    zones_x, zones_y,
    out, slow, slow_raw, code, rec, wave, table, zones, zone_buf, zone_rows, trig, rotated, inline,
    own, sent, got, total,
    local_sems, zone_send, zone_recv, slow_send, slow_recv, fwd_send, fwd_recv,
    rec_send, rec_recv, swap_send, swap_recv, grad_send, grad_recv,
):
    d = lax.axis_index("depth")
    line = lax.axis_index("xline")
    q = lax.rem(line, pair)
    block = line // pair
    mate_line = line + 1 - 2 * q
    width = recv_in.shape[3]
    order = pair * width
    slots = wave.shape[0]
    mine = pl.ds(pl.multiple_of(q * width, width), width)
    theirs = pl.ds(pl.multiple_of((1 - q) * width, width), width)

    def rows_of(section):
        return pl.ds(pl.multiple_of(section * order, order), order)

    barrier = pltpu.get_barrier_semaphore()
    pl.semaphore_signal(barrier, inc=1, device_id=(d, mate_line), device_id_type=MESH)
    others = [lax.rem(d + k, sections) for k in range(1, sections)]
    for other in others:
        pl.semaphore_signal(barrier, inc=1, device_id=(other, line), device_id_type=MESH)

    freqs = pl.ds(q * slots, slots)
    local = [
        pltpu.make_async_copy(
            slow_in.at[0], slow_raw, local_sems.at[0]
        ),
        pltpu.make_async_copy(
            recv_in.at[freqs, :, rows_of(d), :], rec.at[:, :, :, mine], local_sems.at[1]
        ),
        pltpu.make_async_copy(table_in.at[freqs], table, local_sems.at[2]),
    ]
    for copy in local:
        copy.start()
    zones[...] = jnp.zeros_like(zones)
    zones[0:1, 0:zones_x.shape[1]] = zones_x[...]
    zones[1:2, 0:zones_y.shape[1]] = zones_y[...]
    zone_buf[d] = zones[...]
    local[0].wait()
    for start in range(0, slow_raw.shape[0], order):
        part = slice(start, start + order)
        scaled = (slow_raw[part, :] - SLOW_MID) * (1.0 / CODE_STEP)
        code[part, :] = jnp.round(scaled).astype(jnp.int32).astype(jnp.int16)
    slow[d, :, mine] = code[rows_of(d), :]
    pl.semaphore_wait(barrier, sections)

    zone_copies, slow_copies = [], []
    for k, other in enumerate(others):
        zone_copies.append(
            pltpu.make_async_remote_copy(
                src_ref=zones, dst_ref=zone_buf.at[d], send_sem=zone_send.at[k],
                recv_sem=zone_recv.at[d], device_id=(other, line), device_id_type=MESH,
            )
        )
        slow_copies.append(
            pltpu.make_async_remote_copy(
                src_ref=code.at[rows_of(other), :], dst_ref=slow.at[d, :, mine],
                send_sem=slow_send.at[k], recv_sem=slow_recv.at[d],
                device_id=(other, line), device_id_type=MESH,
            )
        )
    for copy in zone_copies + slow_copies:
        copy.start()
    rec_copy = pltpu.make_async_remote_copy(
        src_ref=recv_in.at[pl.ds((1 - q) * slots, slots), :, rows_of(d), :],
        dst_ref=rec.at[:, :, :, mine], send_sem=rec_send, recv_sem=rec_recv,
        device_id=(d, mate_line), device_id_type=MESH,
    )
    rec_copy.start()

    points = src_x.shape[1]
    cells = lax.broadcasted_iota(jnp.int32, (order, points), 0)
    hit_x = cells + d * order == src_x[...]
    hit_y = jnp.where(cells + block * order == src_y[...], 1.0, 0.0).astype(BF16)
    for slot in range(slots):
        for part in range(2):
            amps = amp[q * slots + slot, pl.ds(part, 1), :].astype(F32)
            spread = jnp.where(hit_x, amps, 0.0).astype(BF16)
            field = lax.dot_general(
                spread, hit_y, (((1,), (1,)), ((), ())), preferred_element_type=F32
            )
            wave[slot, 0, part] = field.astype(BF16)

    def arrived_slow(level):
        return pltpu.make_async_remote_copy(
            src_ref=slow.at[level, :, mine], dst_ref=slow.at[level, :, mine],
            send_sem=slow_send.at[0], recv_sem=slow_recv.at[level],
            device_id=(d, mate_line), device_id_type=MESH,
        )

    def forward(level, half):
        return pltpu.make_async_remote_copy(
            src_ref=slow.at[level, :, half], dst_ref=slow.at[level, :, half],
            send_sem=fwd_send.at[level], recv_sem=fwd_recv.at[level],
            device_id=(d, mate_line), device_id_type=MESH,
        )

    def relay(level):
        @pl.when(level != d)
        def _():
            arrived_slow(level).wait_recv()

        forward(level, mine).start()

    relay(0)

    local[1].wait()
    rec_copy.wait_recv()
    for slot in range(slots):
        wave[slot, 1, 0] = rec[slot, 0]
        wave[slot, 1, 1] = -rec[slot, 1]
    local[2].wait()
    for level in range(sections):
        @pl.when(level != d)
        def _():
            pltpu.make_async_remote_copy(
                src_ref=zones, dst_ref=zone_buf.at[level], send_sem=zone_send.at[0],
                recv_sem=zone_recv.at[level], device_id=(d, mate_line), device_id_type=MESH,
            ).wait_recv()
    zone_copy = pltpu.make_async_copy(zone_buf, zone_rows, local_sems.at[3])
    zone_copy.start()
    zone_copy.wait()
    forward(0, theirs).wait_recv()

    def turn(level, slot):
        omega = omegas[q * slots + slot]
        slope = omega * (0.5 * CODE_STEP)
        shift = omega * (0.5 * SLOW_MID) - 0.5 * math.pi
        for start in range(0, order, rows):
            part = slice(start, start + rows)
            value = slow[level, part, :].astype(jnp.int32).astype(F32)
            sine, cosine = sincos(value * slope + shift)
            trig[level % 2, slot, 0, part, :] = sine
            trig[level % 2, slot, 1, part, :] = cosine

    def rotate(level, slot):
        for start in range(0, order, rows):
            part = slice(start, start + rows)
            sine, cosine = trig[level % 2, slot, 0, part, :], trig[level % 2, slot, 1, part, :]
            for field in range(2):
                real = wave[slot, field, 0, part, :].astype(F32)
                imag = wave[slot, field, 1, part, :].astype(F32)
                lanes = slice(field * order, (field + 1) * order)
                rotated[slot, part, lanes] = (real * cosine - imag * sine).astype(BF16)
                rotated[slot, order + start:order + start + rows, lanes] = (
                    real * sine + imag * cosine
                ).astype(BF16)

    def solve_inline(level, slot):
        m_x = block_form(table[slot, zone_rows[level, 0, d]])
        for field in range(2):
            lanes = slice(field * order, (field + 1) * order)
            value = rotated[slot, :, lanes]
            solved = value.astype(F32) + jnp.dot(m_x, value, preferred_element_type=F32)
            solved = solved.astype(BF16)
            inline[slot, lanes, 0:order] = solved[:order]
            inline[slot, lanes, order:] = solved[order:]

    def solve_crossline(level, slot):
        omega = omegas[q * slots + slot]
        m_y = block_form(table[slot, zone_rows[level, 1, block]])
        value = inline[slot]
        product = []
        for part in range(2):
            lanes = slice(part * order, (part + 1) * order)
            solved = value[:, lanes].astype(F32) + lax.dot_general(
                value, m_y[lanes], (((1,), (1,)), ((), ())), preferred_element_type=F32
            )
            solved = solved.astype(BF16)
            wave[slot, 0, part] = solved[:order]
            wave[slot, 1, part] = solved[order:]
            product.append(solved[:order].astype(F32) * solved[order:].astype(F32))
        image = (omega * omega) * (product[0] - product[1])
        if slot == 0:
            total[...] = image
        else:
            total[...] += image

    def swap(level):
        return pltpu.make_async_remote_copy(
            src_ref=sent.at[level], dst_ref=got.at[level],
            send_sem=swap_send.at[level], recv_sem=swap_recv.at[level],
            device_id=(d, mate_line), device_id_type=MESH,
        )

    def deliver_copy(level):
        return pltpu.make_async_remote_copy(
            src_ref=own.at[level], dst_ref=out.at[rows_of(d), :],
            send_sem=grad_send.at[level], recv_sem=grad_recv.at[d],
            device_id=(level, line), device_id_type=MESH,
        )

    def deliver(level):
        swap(level).wait_recv()
        both = own[level].astype(F32) + got[level].astype(F32)

        @pl.when(level == d)
        def _():
            out[rows_of(d), :] = both.astype(BF16)

        @pl.when(level != d)
        def _():
            own[level] = both.astype(BF16)
            deliver_copy(level).start()

    for level in range(sections):
        if level + 1 < sections:
            relay(level + 1)
            if level > 0:
                forward(level + 1, theirs).wait_recv()
        if level > 0:
            deliver(level - 1)
        if level < 2:
            for slot in range(slots):
                turn(level, slot)
        for stage in (rotate, solve_inline, solve_crossline):
            for slot in range(slots):
                stage(level, slot)
        if 0 < level < sections - 1:
            for slot in range(slots):
                turn(level + 1, slot)
        own[level] = total[:, mine].astype(BF16)
        sent[level] = total[:, theirs].astype(BF16)
        swap(level).start()
        if level == 0:
            forward(1, theirs).wait_recv()
    deliver(sections - 1)

    for copy in zone_copies + slow_copies:
        copy.wait_send()
    rec_copy.wait_send()
    for level in range(sections):
        forward(level, mine).wait_send()
        swap(level).wait_send()

        @pl.when(level != d)
        def _():
            deliver_copy(level).wait_send()
            pltpu.make_async_remote_copy(
                src_ref=own.at[level], dst_ref=out.at[rows_of(level), :],
                send_sem=grad_send.at[0], recv_sem=grad_recv.at[level],
                device_id=(level, line), device_id_type=MESH,
            ).wait_recv()


def per_device(
    receiver_data, source_amp, source_x, source_y, omegas, slowness, inverses, zones_x, zones_y
):
    sections = lax.axis_size("depth")
    freqs, _, width_x, width_y = receiver_data.shape
    order = inverses.shape[-1]
    pair = order // width_y
    points = source_x.shape[0]
    zone_count = inverses.shape[1]
    slots = freqs // pair
    assert pair == 2 and width_x == order * sections and slowness.shape[0] == 1
    vmem = pl.BlockSpec(memory_space=pltpu.VMEM)
    smem = pl.BlockSpec(memory_space=pltpu.SMEM)
    anywhere = pl.BlockSpec(memory_space=pl.ANY)
    dma = pltpu.SemaphoreType.DMA
    out = pl.pallas_call(
        functools.partial(kernel, sections, pair, 32),
        out_shape=jax.ShapeDtypeStruct((width_x, width_y), BF16),
        in_specs=[anywhere, vmem, vmem, vmem, smem, anywhere, anywhere, vmem, vmem],
        out_specs=vmem,
        scratch_shapes=[
            pltpu.VMEM((sections, order, order), jnp.int16),
            pltpu.VMEM((width_x, width_y), F32),
            pltpu.VMEM((width_x, width_y), jnp.int16),
            pltpu.VMEM((slots, 2, order, order), BF16),
            pltpu.VMEM((slots, 2, 2, order, order), BF16),
            pltpu.VMEM((slots, zone_count, 2, order, order), BF16),
            pltpu.VMEM((8, 128), jnp.int32),
            pltpu.VMEM((sections, 8, 128), jnp.int32),
            pltpu.SMEM((sections, 8, 128), jnp.int32),
            pltpu.VMEM((2, slots, 2, order, order), F32),
            pltpu.VMEM((slots, 2 * order, 2 * order), BF16),
            pltpu.VMEM((slots, 2 * order, 2 * order), BF16),
            pltpu.VMEM((sections, order, width_y), BF16),
            pltpu.VMEM((sections, order, width_y), BF16),
            pltpu.VMEM((sections, order, width_y), BF16),
            pltpu.VMEM((order, order), F32),
            dma((4,)),
            dma((sections,)), dma((sections,)),
            dma((sections,)), dma((sections,)),
            dma((sections,)), dma((sections,)),
            dma, dma,
            dma((sections,)), dma((sections,)),
            dma((sections,)), dma((sections,)),
        ],
        compiler_params=pltpu.CompilerParams(collective_id=0, has_side_effects=True),
    )(
        receiver_data, source_amp, source_x.reshape(1, points), source_y.reshape(1, points),
        omegas, slowness, inverses, zones_x, zones_y,
    )
    return out.astype(F32)[None]


def solution(mesh):
    in_specs = (
        P(None, None, None, "xline"),
        P(),
        P(),
        P(),
        P(),
        P("depth", None, "xline"),
        P(),
        P("depth", None),
        P("depth", None),
    )
    out_specs = P("depth", None, "xline")
    return jax.shard_map(
        per_device, mesh=mesh, in_specs=in_specs, out_specs=out_specs, check_vma=False
    )
```

```python
import functools
import math

import jax
import jax.numpy as jnp
import numpy as np
from jax import lax
from jax.experimental import pallas as pl
from jax.experimental.pallas import tpu as pltpu
from jax.sharding import PartitionSpec as P

MESH = pl.DeviceIdType.MESH
F32 = jnp.float32
BF16 = jnp.bfloat16

SLOW_LOW, SLOW_HIGH = 0.2, 2.0
OMEGA_LOW, OMEGA_HIGH = 0.5, 3.0
SLOW_MID = 0.5 * (SLOW_LOW + SLOW_HIGH)
CODE_STEP = (SLOW_HIGH - SLOW_LOW) / 65532.0
HALF_SPAN = 0.5 * max(OMEGA_HIGH * SLOW_HIGH - math.pi, math.pi - OMEGA_LOW * SLOW_LOW) + 0.01


def fitted(function, count):
    nodes = np.cos(np.pi * (np.arange(64) + 0.5) / 64)
    square = 0.5 * HALF_SPAN**2 * (nodes + 1.0)
    fit = np.polynomial.Chebyshev.fit(square, function(np.sqrt(square)), count - 1)
    return [float(term) for term in fit.convert(kind=np.polynomial.Polynomial).coef]


ROOT2 = math.sqrt(2.0)
SIN_TERMS = fitted(lambda t: ROOT2 * np.sin(t) / t, 5)
COS_TERMS = fitted(lambda t: -ROOT2 * np.cos(t), 5)


def series(square, terms):
    total = square * terms[-1] + terms[-2]
    for term in terms[-3::-1]:
        total = total * square + term
    return total


def sincos(half):
    square = half * half
    root_sine = series(square, SIN_TERMS) * half
    return root_sine * series(square, COS_TERMS), root_sine * root_sine - 1.0


def block_form(blocks):
    k_real, k_imag = blocks[0], blocks[1]
    top = jnp.concatenate([k_real, -k_imag], axis=1)
    bottom = jnp.concatenate([k_imag, k_real], axis=1)
    return jnp.concatenate([top, bottom], axis=0)


def kernel(
    sections, pair, rows, recv_in, amp, src_x, src_y, omegas, slow_in, table_in,
    zones_x, zones_y,
    out, slow, slow_raw, code, rec, wave, table, zones, zone_buf, zone_rows, trig, rotated, inline,
    own, sent, got, total,
    local_sems, zone_send, zone_recv, slow_send, slow_recv, fwd_send, fwd_recv,
    rec_send, rec_recv, swap_send, swap_recv, grad_send, grad_recv,
):
    d = lax.axis_index("depth")
    line = lax.axis_index("xline")
    q = lax.rem(line, pair)
    block = line // pair
    mate_line = line + 1 - 2 * q
    width = recv_in.shape[3]
    order = pair * width
    slots = wave.shape[0]
    mine = pl.ds(pl.multiple_of(q * width, width), width)
    theirs = pl.ds(pl.multiple_of((1 - q) * width, width), width)

    def rows_of(section):
        return pl.ds(pl.multiple_of(section * order, order), order)

    barrier = pltpu.get_barrier_semaphore()
    pl.semaphore_signal(barrier, inc=1, device_id=(d, mate_line), device_id_type=MESH)
    others = [lax.rem(d + k, sections) for k in range(1, sections)]
    for other in others:
        pl.semaphore_signal(barrier, inc=1, device_id=(other, line), device_id_type=MESH)

    freqs = pl.ds(q * slots, slots)
    local = [
        pltpu.make_async_copy(
            slow_in.at[0], slow_raw, local_sems.at[0]
        ),
        pltpu.make_async_copy(
            recv_in.at[freqs, :, rows_of(d), :], rec.at[:, :, :, mine], local_sems.at[1]
        ),
        pltpu.make_async_copy(table_in.at[freqs], table, local_sems.at[2]),
    ]
    for copy in local:
        copy.start()
    zones[...] = jnp.zeros_like(zones)
    zones[0:1, 0:zones_x.shape[1]] = zones_x[...]
    zones[1:2, 0:zones_y.shape[1]] = zones_y[...]
    zone_buf[d] = zones[...]
    local[0].wait()
    for start in range(0, slow_raw.shape[0], order):
        part = slice(start, start + order)
        scaled = (slow_raw[part, :] - SLOW_MID) * (1.0 / CODE_STEP)
        code[part, :] = jnp.round(scaled).astype(jnp.int32).astype(jnp.int16)
    slow[d, :, mine] = code[rows_of(d), :]
    pl.semaphore_wait(barrier, sections)

    zone_copies, slow_copies = [], []
    for k, other in enumerate(others):
        zone_copies.append(
            pltpu.make_async_remote_copy(
                src_ref=zones, dst_ref=zone_buf.at[d], send_sem=zone_send.at[k],
                recv_sem=zone_recv.at[d], device_id=(other, line), device_id_type=MESH,
            )
        )
        slow_copies.append(
            pltpu.make_async_remote_copy(
                src_ref=code.at[rows_of(other), :], dst_ref=slow.at[d, :, mine],
                send_sem=slow_send.at[k], recv_sem=slow_recv.at[d],
                device_id=(other, line), device_id_type=MESH,
            )
        )
    for copy in zone_copies + slow_copies:
        copy.start()
    rec_copy = pltpu.make_async_remote_copy(
        src_ref=recv_in.at[pl.ds((1 - q) * slots, slots), :, rows_of(d), :],
        dst_ref=rec.at[:, :, :, mine], send_sem=rec_send, recv_sem=rec_recv,
        device_id=(d, mate_line), device_id_type=MESH,
    )
    rec_copy.start()

    def arrived_slow(level):
        return pltpu.make_async_remote_copy(
            src_ref=slow.at[level, :, mine], dst_ref=slow.at[level, :, mine],
            send_sem=slow_send.at[0], recv_sem=slow_recv.at[level],
            device_id=(d, mate_line), device_id_type=MESH,
        )

    def forward(level, half):
        return pltpu.make_async_remote_copy(
            src_ref=slow.at[level, :, half], dst_ref=slow.at[level, :, half],
            send_sem=fwd_send.at[level], recv_sem=fwd_recv.at[level],
            device_id=(d, mate_line), device_id_type=MESH,
        )

    def turn(level, lanes):
        for slot in range(slots):
            omega = omegas[q * slots + slot]
            slope = omega * (0.5 * CODE_STEP)
            shift = omega * (0.5 * SLOW_MID) - 0.5 * math.pi
            for start in range(0, order, rows):
                part = slice(start, start + rows)
                value = slow[level, part, lanes].astype(jnp.int32).astype(F32)
                sine, cosine = sincos(value * slope + shift)
                trig[level, slot, 0, part, lanes] = sine
                trig[level, slot, 1, part, lanes] = cosine

    forward(d, mine).start()

    points = src_x.shape[1]
    cells = lax.broadcasted_iota(jnp.int32, (order, points), 0)
    hit_x = cells + d * order == src_x[...]
    hit_y = jnp.where(cells + block * order == src_y[...], 1.0, 0.0).astype(BF16)
    for slot in range(slots):
        for part in range(2):
            amps = amp[q * slots + slot, pl.ds(part, 1), :].astype(F32)
            spread = jnp.where(hit_x, amps, 0.0).astype(BF16)
            field = lax.dot_general(
                spread, hit_y, (((1,), (1,)), ((), ())), preferred_element_type=F32
            )
            wave[slot, 0, part] = field.astype(BF16)

    local[1].wait()
    rec_copy.wait_recv()
    for slot in range(slots):
        wave[slot, 1, 0] = rec[slot, 0]
        wave[slot, 1, 1] = -rec[slot, 1]
    local[2].wait()
    forward(d, theirs).wait_recv()
    turn(d, slice(0, order))
    for level in range(sections):
        @pl.when(level != d)
        def _():
            pltpu.make_async_remote_copy(
                src_ref=zones, dst_ref=zone_buf.at[level], send_sem=zone_send.at[0],
                recv_sem=zone_recv.at[level], device_id=(d, mate_line), device_id_type=MESH,
            ).wait_recv()
    zone_copy = pltpu.make_async_copy(zone_buf, zone_rows, local_sems.at[3])
    zone_copy.start()
    zone_copy.wait()

    @pl.when(d != 0)
    def _():
        arrived_slow(0).wait_recv()
        forward(0, mine).start()
        turn(0, mine)
        forward(0, theirs).wait_recv()
        turn(0, theirs)

    def rotate(level, slot):
        for start in range(0, order, rows):
            part = slice(start, start + rows)
            sine, cosine = trig[level, slot, 0, part, :], trig[level, slot, 1, part, :]
            for field in range(2):
                real = wave[slot, field, 0, part, :].astype(F32)
                imag = wave[slot, field, 1, part, :].astype(F32)
                lanes = slice(field * order, (field + 1) * order)
                rotated[slot, part, lanes] = (real * cosine - imag * sine).astype(BF16)
                rotated[slot, order + start:order + start + rows, lanes] = (
                    real * sine + imag * cosine
                ).astype(BF16)

    def solve_inline(level, slot):
        m_x = block_form(table[slot, zone_rows[level, 0, d]])
        for field in range(2):
            lanes = slice(field * order, (field + 1) * order)
            value = rotated[slot, :, lanes]
            solved = value.astype(F32) + jnp.dot(m_x, value, preferred_element_type=F32)
            solved = solved.astype(BF16)
            inline[slot, lanes, 0:order] = solved[:order]
            inline[slot, lanes, order:] = solved[order:]

    def solve_crossline(level, slot):
        omega = omegas[q * slots + slot]
        m_y = block_form(table[slot, zone_rows[level, 1, block]])
        value = inline[slot]
        product = []
        for part in range(2):
            lanes = slice(part * order, (part + 1) * order)
            solved = value[:, lanes].astype(F32) + lax.dot_general(
                value, m_y[lanes], (((1,), (1,)), ((), ())), preferred_element_type=F32
            )
            product.append(solved[:order] * solved[order:])
            if level + 1 < sections:
                wave[slot, 0, part] = solved[:order].astype(BF16)
                wave[slot, 1, part] = solved[order:].astype(BF16)
        image = (omega * omega) * (product[0] - product[1])
        if slot == 0:
            total[...] = image
        else:
            total[...] += image

    def swap(level):
        return pltpu.make_async_remote_copy(
            src_ref=sent.at[level], dst_ref=got.at[level],
            send_sem=swap_send.at[level], recv_sem=swap_recv.at[level],
            device_id=(d, mate_line), device_id_type=MESH,
        )

    def deliver_copy(level):
        return pltpu.make_async_remote_copy(
            src_ref=own.at[level], dst_ref=out.at[rows_of(d), :],
            send_sem=grad_send.at[level], recv_sem=grad_recv.at[d],
            device_id=(level, line), device_id_type=MESH,
        )

    def deliver(level):
        swap(level).wait_recv()
        both = own[level].astype(F32) + got[level].astype(F32)

        @pl.when(level == d)
        def _():
            out[rows_of(d), :] = both.astype(BF16)

        @pl.when(level != d)
        def _():
            own[level] = both.astype(BF16)
            deliver_copy(level).start()

    for level in range(sections):
        if level > 0:
            @pl.when(level != d)
            def _():
                forward(level, theirs).wait_recv()
                turn(level, slice(0, order))

        if level + 1 < sections:
            @pl.when(level + 1 != d)
            def _():
                arrived_slow(level + 1).wait_recv()
                forward(level + 1, mine).start()

        if level > 0:
            deliver(level - 1)
        for stage in (rotate, solve_inline, solve_crossline):
            for slot in range(slots):
                stage(level, slot)
        own[level] = total[:, mine].astype(BF16)
        sent[level] = total[:, theirs].astype(BF16)
        swap(level).start()
    deliver(sections - 1)

    for copy in zone_copies + slow_copies:
        copy.wait_send()
    rec_copy.wait_send()
    for level in range(sections):
        forward(level, mine).wait_send()
        swap(level).wait_send()

        @pl.when(level != d)
        def _():
            deliver_copy(level).wait_send()
            pltpu.make_async_remote_copy(
                src_ref=own.at[level], dst_ref=out.at[rows_of(level), :],
                send_sem=grad_send.at[0], recv_sem=grad_recv.at[level],
                device_id=(level, line), device_id_type=MESH,
            ).wait_recv()


def per_device(
    receiver_data, source_amp, source_x, source_y, omegas, slowness, inverses, zones_x, zones_y
):
    sections = lax.axis_size("depth")
    freqs, _, width_x, width_y = receiver_data.shape
    order = inverses.shape[-1]
    pair = order // width_y
    points = source_x.shape[0]
    zone_count = inverses.shape[1]
    slots = freqs // pair
    assert pair == 2 and width_x == order * sections and slowness.shape[0] == 1
    vmem = pl.BlockSpec(memory_space=pltpu.VMEM)
    smem = pl.BlockSpec(memory_space=pltpu.SMEM)
    anywhere = pl.BlockSpec(memory_space=pl.ANY)
    dma = pltpu.SemaphoreType.DMA
    out = pl.pallas_call(
        functools.partial(kernel, sections, pair, 32),
        out_shape=pltpu.VMEM((width_x, width_y), BF16),
        in_specs=[anywhere, vmem, vmem, vmem, smem, anywhere, anywhere, vmem, vmem],
        out_specs=vmem,
        scratch_shapes=[
            pltpu.VMEM((sections, order, order), jnp.int16),
            pltpu.VMEM((width_x, width_y), F32),
            pltpu.VMEM((width_x, width_y), jnp.int16),
            pltpu.VMEM((slots, 2, order, order), BF16),
            pltpu.VMEM((slots, 2, 2, order, order), BF16),
            pltpu.VMEM((slots, zone_count, 2, order, order), BF16),
            pltpu.VMEM((8, 128), jnp.int32),
            pltpu.VMEM((sections, 8, 128), jnp.int32),
            pltpu.SMEM((sections, 8, 128), jnp.int32),
            pltpu.VMEM((sections, slots, 2, order, order), F32),
            pltpu.VMEM((slots, 2 * order, 2 * order), BF16),
            pltpu.VMEM((slots, 2 * order, 2 * order), BF16),
            pltpu.VMEM((sections, order, width_y), BF16),
            pltpu.VMEM((sections, order, width_y), BF16),
            pltpu.VMEM((sections, order, width_y), BF16),
            pltpu.VMEM((order, order), F32),
            dma((4,)),
            dma((sections,)), dma((sections,)),
            dma((sections,)), dma((sections,)),
            dma((sections,)), dma((sections,)),
            dma, dma,
            dma((sections,)), dma((sections,)),
            dma((sections,)), dma((sections,)),
        ],
        compiler_params=pltpu.CompilerParams(collective_id=0, has_side_effects=True),
    )(
        receiver_data, source_amp, source_x.reshape(1, points), source_y.reshape(1, points),
        omegas, slowness, inverses, zones_x, zones_y,
    )
    return out.astype(F32)[None]


def solution(mesh):
    in_specs = (
        P(None, None, None, "xline"),
        P(),
        P(),
        P(),
        P(),
        P("depth", None, "xline"),
        P(),
        P("depth", None),
        P("depth", None),
    )
    out_specs = P("depth", None, "xline")
    return jax.shard_map(
        per_device, mesh=mesh, in_specs=in_specs, out_specs=out_specs, check_vma=False
    )
```

```python
import functools
import math

import jax
import jax.numpy as jnp
import numpy as np
from jax import lax
from jax.experimental import pallas as pl
from jax.experimental.pallas import tpu as pltpu
from jax.sharding import PartitionSpec as P

MESH = pl.DeviceIdType.MESH
F32 = jnp.float32
BF16 = jnp.bfloat16

SLOW_LOW, SLOW_HIGH = 0.2, 2.0
OMEGA_LOW, OMEGA_HIGH = 0.5, 3.0
SLOW_MID = 0.5 * (SLOW_LOW + SLOW_HIGH)
CODE_STEP = (SLOW_HIGH - SLOW_LOW) / 65532.0
HALF_SPAN = 0.5 * max(OMEGA_HIGH * SLOW_HIGH - math.pi, math.pi - OMEGA_LOW * SLOW_LOW) + 0.01


def fitted(function, count):
    nodes = np.cos(np.pi * (np.arange(64) + 0.5) / 64)
    square = 0.5 * HALF_SPAN**2 * (nodes + 1.0)
    fit = np.polynomial.Chebyshev.fit(square, function(np.sqrt(square)), count - 1)
    return [float(term) for term in fit.convert(kind=np.polynomial.Polynomial).coef]


ROOT2 = math.sqrt(2.0)
SIN_TERMS = fitted(lambda t: ROOT2 * np.sin(t) / t, 5)
COS_TERMS = fitted(lambda t: -ROOT2 * np.cos(t), 5)


def series(square, terms):
    total = square * terms[-1] + terms[-2]
    for term in terms[-3::-1]:
        total = total * square + term
    return total


def sincos(half):
    square = half * half
    root_sine = series(square, SIN_TERMS) * half
    return root_sine * series(square, COS_TERMS), root_sine * root_sine - 1.0


def block_form(blocks):
    k_real, k_imag = blocks[0], blocks[1]
    top = jnp.concatenate([k_real, -k_imag], axis=1)
    bottom = jnp.concatenate([k_imag, k_real], axis=1)
    return jnp.concatenate([top, bottom], axis=0)


def flip(index, bits):
    for bit in (1, 2, 4, 8):
        if bits & bit:
            index = index + bit - 2 * bit * lax.rem(index // bit, 2)
    return index


def kernel(
    sections, pair, rows, recv_in, amp, src_x, src_y, omegas, slow_in, table_in,
    zones_x, zones_y,
    out, slow, slow_raw, code, rec, wave, table, zones, zone_buf, zone_rows, trig, rotated, inline,
    own, sent, got, total,
    local_sems, zone_send, zone_recv, slow_send, slow_recv, fwd_send, fwd_recv,
    rec_send, rec_recv, swap_send, swap_recv, grad_send, grad_recv,
):
    d = lax.axis_index("depth")
    line = lax.axis_index("xline")
    q = lax.rem(line, pair)
    block = line // pair
    mate_line = line + 1 - 2 * q
    width = recv_in.shape[3]
    order = pair * width
    slots = wave.shape[0]
    mine = pl.ds(pl.multiple_of(q * width, width), width)
    theirs = pl.ds(pl.multiple_of((1 - q) * width, width), width)

    def rows_of(section):
        return pl.ds(pl.multiple_of(section * order, order), order)

    barrier = pltpu.get_barrier_semaphore()
    pl.semaphore_signal(barrier, inc=1, device_id=(d, mate_line), device_id_type=MESH)
    others = [flip(d, k) for k in range(1, sections)]
    for other in others:
        pl.semaphore_signal(barrier, inc=1, device_id=(other, line), device_id_type=MESH)

    freqs = pl.ds(q * slots, slots)
    local = [
        pltpu.make_async_copy(
            slow_in.at[0], slow_raw, local_sems.at[0]
        ),
        pltpu.make_async_copy(
            recv_in.at[freqs, :, rows_of(d), :], rec.at[:, :, :, mine], local_sems.at[1]
        ),
        pltpu.make_async_copy(table_in.at[freqs], table, local_sems.at[2]),
    ]
    for copy in local:
        copy.start()
    zones[...] = jnp.zeros_like(zones)
    zones[0:1, 0:zones_x.shape[1]] = zones_x[...]
    zones[1:2, 0:zones_y.shape[1]] = zones_y[...]
    zone_buf[d] = zones[...]
    local[0].wait()
    for start in range(0, slow_raw.shape[0], order):
        part = slice(start, start + order)
        scaled = (slow_raw[part, :] - SLOW_MID) * (1.0 / CODE_STEP)
        code[part, :] = jnp.round(scaled).astype(jnp.int32).astype(jnp.int16)
    slow[d, :, mine] = code[rows_of(d), :]
    pl.semaphore_wait(barrier, sections)

    zone_copies, slow_copies = [], []
    for k, other in enumerate(others):
        zone_copies.append(
            pltpu.make_async_remote_copy(
                src_ref=zones, dst_ref=zone_buf.at[d], send_sem=zone_send.at[k],
                recv_sem=zone_recv.at[d], device_id=(other, line), device_id_type=MESH,
            )
        )
        slow_copies.append(
            pltpu.make_async_remote_copy(
                src_ref=code.at[rows_of(other), :], dst_ref=slow.at[d, :, mine],
                send_sem=slow_send.at[k], recv_sem=slow_recv.at[d],
                device_id=(other, line), device_id_type=MESH,
            )
        )
    for copy in zone_copies + slow_copies:
        copy.start()
    rec_copy = pltpu.make_async_remote_copy(
        src_ref=recv_in.at[pl.ds((1 - q) * slots, slots), :, rows_of(d), :],
        dst_ref=rec.at[:, :, :, mine], send_sem=rec_send, recv_sem=rec_recv,
        device_id=(d, mate_line), device_id_type=MESH,
    )
    rec_copy.start()

    def arrived_slow(level):
        return pltpu.make_async_remote_copy(
            src_ref=slow.at[level, :, mine], dst_ref=slow.at[level, :, mine],
            send_sem=slow_send.at[0], recv_sem=slow_recv.at[level],
            device_id=(d, mate_line), device_id_type=MESH,
        )

    def forward(level, half):
        return pltpu.make_async_remote_copy(
            src_ref=slow.at[level, :, half], dst_ref=slow.at[level, :, half],
            send_sem=fwd_send.at[level], recv_sem=fwd_recv.at[level],
            device_id=(d, mate_line), device_id_type=MESH,
        )

    def turn(level, lanes):
        for slot in range(slots):
            omega = omegas[q * slots + slot]
            slope = omega * (0.5 * CODE_STEP)
            shift = omega * (0.5 * SLOW_MID) - 0.5 * math.pi
            for start in range(0, order, rows):
                part = slice(start, start + rows)
                value = slow[level, part, lanes].astype(jnp.int32).astype(F32)
                sine, cosine = sincos(value * slope + shift)
                trig[level, slot, 0, part, lanes] = sine
                trig[level, slot, 1, part, lanes] = cosine

    forward(d, mine).start()

    points = src_x.shape[1]
    cells = lax.broadcasted_iota(jnp.int32, (order, points), 0)
    hit_x = cells + d * order == src_x[...]
    hit_y = jnp.where(cells + block * order == src_y[...], 1.0, 0.0).astype(BF16)
    for slot in range(slots):
        for part in range(2):
            amps = amp[q * slots + slot, pl.ds(part, 1), :].astype(F32)
            spread = jnp.where(hit_x, amps, 0.0).astype(BF16)
            field = lax.dot_general(
                spread, hit_y, (((1,), (1,)), ((), ())), preferred_element_type=F32
            )
            wave[slot, 0, part] = field.astype(BF16)

    local[1].wait()
    rec_copy.wait_recv()
    for slot in range(slots):
        wave[slot, 1, 0] = rec[slot, 0]
        wave[slot, 1, 1] = -rec[slot, 1]
    local[2].wait()
    forward(d, theirs).wait_recv()
    turn(d, slice(0, order))
    for level in range(sections):
        @pl.when(level != d)
        def _():
            pltpu.make_async_remote_copy(
                src_ref=zones, dst_ref=zone_buf.at[level], send_sem=zone_send.at[0],
                recv_sem=zone_recv.at[level], device_id=(d, mate_line), device_id_type=MESH,
            ).wait_recv()
    zone_copy = pltpu.make_async_copy(zone_buf, zone_rows, local_sems.at[3])
    zone_copy.start()
    zone_copy.wait()

    def rotate(level, slot, base=0, size=order):
        near = pl.ds(base, size) if size == order else pl.ds(pl.multiple_of(base, size), size)
        for start in range(0, order, rows):
            part = slice(start, start + rows)
            sine, cosine = trig[level, slot, 0, part, near], trig[level, slot, 1, part, near]
            for field in range(2):
                real = wave[slot, field, 0, part, near].astype(F32)
                imag = wave[slot, field, 1, part, near].astype(F32)
                if size == order:
                    lanes = pl.ds(field * order, order)
                else:
                    lanes = pl.ds(pl.multiple_of(field * order + base, size), size)
                rotated[slot, part, lanes] = (real * cosine - imag * sine).astype(BF16)
                rotated[slot, order + start:order + start + rows, lanes] = (
                    real * sine + imag * cosine
                ).astype(BF16)

    @pl.when(d == 0)
    def _():
        for slot in range(slots):
            rotate(0, slot, q * width, width)

    @pl.when(d != 0)
    def _():
        arrived_slow(0).wait_recv()
        forward(0, mine).start()
        turn(0, mine)
        for slot in range(slots):
            rotate(0, slot, q * width, width)
        forward(0, theirs).wait_recv()
        turn(0, theirs)

    def solve_inline(level, slot):
        m_x = block_form(table[slot, zone_rows[level, 0, d]])
        for field in range(2):
            lanes = slice(field * order, (field + 1) * order)
            value = rotated[slot, :, lanes]
            solved = value.astype(F32) + jnp.dot(m_x, value, preferred_element_type=F32)
            solved = solved.astype(BF16)
            inline[slot, lanes, 0:order] = solved[:order]
            inline[slot, lanes, order:] = solved[order:]

    def solve_crossline(level, slot):
        omega = omegas[q * slots + slot]
        m_y = block_form(table[slot, zone_rows[level, 1, block]])
        value = inline[slot]
        product = []
        for part in range(2):
            lanes = slice(part * order, (part + 1) * order)
            solved = value[:, lanes].astype(F32) + lax.dot_general(
                value, m_y[lanes], (((1,), (1,)), ((), ())), preferred_element_type=F32
            )
            product.append(solved[:order] * solved[order:])
            if level + 1 < sections:
                wave[slot, 0, part] = solved[:order].astype(BF16)
                wave[slot, 1, part] = solved[order:].astype(BF16)
        image = (omega * omega) * (product[0] - product[1])
        if slot == 0:
            total[...] = image
        else:
            total[...] += image

    def swap(level):
        return pltpu.make_async_remote_copy(
            src_ref=sent.at[level], dst_ref=got.at[level],
            send_sem=swap_send.at[level], recv_sem=swap_recv.at[level],
            device_id=(d, mate_line), device_id_type=MESH,
        )

    def deliver_copy(level):
        return pltpu.make_async_remote_copy(
            src_ref=own.at[level], dst_ref=out.at[rows_of(d), :],
            send_sem=grad_send.at[level], recv_sem=grad_recv.at[d],
            device_id=(level, line), device_id_type=MESH,
        )

    def deliver(level):
        swap(level).wait_recv()
        both = own[level].astype(F32) + got[level].astype(F32)

        @pl.when(level == d)
        def _():
            out[rows_of(d), :] = both.astype(BF16)

        @pl.when(level != d)
        def _():
            own[level] = both.astype(BF16)
            deliver_copy(level).start()

    for level in range(sections):
        if level > 0:
            @pl.when(level != d)
            def _():
                forward(level, theirs).wait_recv()
                turn(level, slice(0, order))

        if level + 1 < sections:
            @pl.when(level + 1 != d)
            def _():
                arrived_slow(level + 1).wait_recv()
                forward(level + 1, mine).start()

        if level > 0:
            deliver(level - 1)
        for slot in range(slots):
            if level == 0:
                rotate(0, slot, (1 - q) * width, width)
            else:
                rotate(level, slot)
        for stage in (solve_inline, solve_crossline):
            for slot in range(slots):
                stage(level, slot)
        own[level] = total[:, mine].astype(BF16)
        sent[level] = total[:, theirs].astype(BF16)
        swap(level).start()
    deliver(sections - 1)

    for copy in zone_copies + slow_copies:
        copy.wait_send()
    rec_copy.wait_send()
    for level in range(sections):
        forward(level, mine).wait_send()
        swap(level).wait_send()

        @pl.when(level != d)
        def _():
            deliver_copy(level).wait_send()
            pltpu.make_async_remote_copy(
                src_ref=own.at[level], dst_ref=out.at[rows_of(level), :],
                send_sem=grad_send.at[0], recv_sem=grad_recv.at[level],
                device_id=(level, line), device_id_type=MESH,
            ).wait_recv()


def per_device(
    receiver_data, source_amp, source_x, source_y, omegas, slowness, inverses, zones_x, zones_y
):
    sections = lax.axis_size("depth")
    freqs, _, width_x, width_y = receiver_data.shape
    order = inverses.shape[-1]
    pair = order // width_y
    points = source_x.shape[0]
    zone_count = inverses.shape[1]
    slots = freqs // pair
    assert pair == 2 and width_x == order * sections and slowness.shape[0] == 1
    assert sections & (sections - 1) == 0
    vmem = pl.BlockSpec(memory_space=pltpu.VMEM)
    smem = pl.BlockSpec(memory_space=pltpu.SMEM)
    anywhere = pl.BlockSpec(memory_space=pl.ANY)
    dma = pltpu.SemaphoreType.DMA
    out = pl.pallas_call(
        functools.partial(kernel, sections, pair, 32),
        out_shape=pltpu.VMEM((width_x, width_y), BF16),
        in_specs=[anywhere, vmem, vmem, vmem, smem, anywhere, anywhere, vmem, vmem],
        out_specs=vmem,
        scratch_shapes=[
            pltpu.VMEM((sections, order, order), jnp.int16),
            pltpu.VMEM((width_x, width_y), F32),
            pltpu.VMEM((width_x, width_y), jnp.int16),
            pltpu.VMEM((slots, 2, order, order), BF16),
            pltpu.VMEM((slots, 2, 2, order, order), BF16),
            pltpu.VMEM((slots, zone_count, 2, order, order), BF16),
            pltpu.VMEM((8, 128), jnp.int32),
            pltpu.VMEM((sections, 8, 128), jnp.int32),
            pltpu.SMEM((sections, 8, 128), jnp.int32),
            pltpu.VMEM((sections, slots, 2, order, order), F32),
            pltpu.VMEM((slots, 2 * order, 2 * order), BF16),
            pltpu.VMEM((slots, 2 * order, 2 * order), BF16),
            pltpu.VMEM((sections, order, width_y), BF16),
            pltpu.VMEM((sections, order, width_y), BF16),
            pltpu.VMEM((sections, order, width_y), BF16),
            pltpu.VMEM((order, order), F32),
            dma((4,)),
            dma((sections,)), dma((sections,)),
            dma((sections,)), dma((sections,)),
            dma((sections,)), dma((sections,)),
            dma, dma,
            dma((sections,)), dma((sections,)),
            dma((sections,)), dma((sections,)),
        ],
        compiler_params=pltpu.CompilerParams(collective_id=0, has_side_effects=True),
    )(
        receiver_data, source_amp, source_x.reshape(1, points), source_y.reshape(1, points),
        omegas, slowness, inverses, zones_x, zones_y,
    )
    return out.astype(F32)[None]


def solution(mesh):
    in_specs = (
        P(None, None, None, "xline"),
        P(),
        P(),
        P(),
        P(),
        P("depth", None, "xline"),
        P(),
        P("depth", None),
        P("depth", None),
    )
    out_specs = P("depth", None, "xline")
    return jax.shard_map(
        per_device, mesh=mesh, in_specs=in_specs, out_specs=out_specs, check_vma=False
    )
```
